1024 devices in a mesh: lat: 16 (over y, x), lev: 64 (over z, core).
Axes of the slice: x: 4, y: 4, z: 32, core: 2. Of those that a mesh axis runs over, the one named last changes fastest.
Arguments:
- adjoint_grid: bfloat16 [128, 768, 1536], P('lev', 'lat'), may hold values from -6 to 6
- wind: bfloat16 [128, 768, 1536], P('lev', 'lat'), may hold values from -6 to 6
- legendre: bfloat16 [1024, 768, 576], P(('lat', 'lev')), may hold values from -0.21875 to 0.21875
- vertical: bfloat16 [16, 128, 128], replicated, may hold values from -0.5 to 0.5
- pair_table: int32 [256], replicated, may hold values from 0 to 255, each once
- degree_matrix: int32 [512], replicated, may hold values from 0 to 15
Outputs:
- adjoint_out: bfloat16 [128, 768, 1536], P('lev', 'lat')
The draws below stay inside these ranges and needn't reach their ends.
Inputs may be any that keep to these rules, and one draw needn't show every extreme that they name: `pair_table`: the values are distinct: every pair (m, 511 - m) with m < 256 stands in exactly one slot.
All inputs are finite; a program needn't handle non-finite values.
Results may differ from the reference program's by a relative error of at most 0.008.
Values may be sent and summed in bfloat16 or wider, within the bound.
A program may use at most 64 MiB of HBM per device.

```python
import math
import jax
import jax.numpy as jnp
from jax import lax

LAT = 768
LON = 1536
LEV = 128
N = 512
NMAT = 16
PAIRS = 256
KP = 576


def plant(entries, key, low, high):
    dims = entries.shape
    index_at = [jax.random.randint(jax.random.fold_in(key, axis), (), 0, dims[axis]) for axis in range(len(dims))]
    entries = entries.at[tuple(index_at)].set(low)
    longest = dims.index(max(dims))
    index_at[longest] = (index_at[longest] + 1) % dims[longest]
    return entries.at[tuple(index_at)].set(high)


def block_scale(key, extent, shards, least, top_value):
    def one(dim, parts):
        heights = jax.random.uniform(jax.random.fold_in(jax.random.fold_in(key, 6), dim), (parts,), jnp.float32, least / len(shards), top_value / len(shards))
        return jnp.repeat(jnp.exp(heights), extent[dim] // parts).reshape((-1,) + (1,) * (len(extent) - dim - 1))

    gain = one(*shards[0])
    for cut in shards[1:]:
        gain = gain * one(*cut)
    return gain


def centred(stream_key, shape, scale, limit, cuts=(), kind=jnp.bfloat16):
    drawn = jax.random.normal(stream_key, shape, jnp.float32) * scale
    if len(cuts) > 0:
        drawn = block_scale(stream_key, shape, cuts, -0.22, 0.18) * drawn
    return jnp.clip(drawn, min=-limit, max=limit).astype(kind)


def setup_inputs(seed: int = 0) -> dict:
    splits = jax.random.split(jax.random.key(seed), 7)
    return {
        "adjoint_grid": centred(splits[0], (LEV, LAT, LON), 1.0, 6.0, ((0, 64), (1, 16))),
        "wind": centred(splits[1], (LEV, LAT, LON), 1.0, 6.0, ((0, 64), (1, 16))),
        "legendre": centred(splits[2], (4 * PAIRS, LAT, KP), LAT ** -0.5, 0.21875, ((0, 1024),)),
        "vertical": centred(splits[3], (NMAT, LEV, LEV), LEV ** -0.5, 0.5),
        "pair_table": jax.random.permutation(splits[4], PAIRS).astype(jnp.int32),
        "degree_matrix": plant(jax.random.randint(splits[5], (N,), 0, NMAT), jax.random.fold_in(splits[5], 1), 0, NMAT - 1).astype(jnp.int32),
    }


def fourier_basis(wavenumbers, points):
    longitude = jnp.arange(points, dtype=jnp.int32)
    phases = wavenumbers[:, :, None] * longitude[None, None, :] % points
    angles = phases.astype(jnp.float32) * (2.0 * jnp.pi / points)
    basis = jnp.stack([jnp.cos(angles), -jnp.sin(angles)], axis=2)
    return basis.reshape(-1, points)

def member_layout(lower_wave, row_start, row_total):
    packed_buffer = row_start + jnp.arange(row_total, dtype=jnp.int32)
    first_member = packed_buffer[None, :] < (N - lower_wave)[:, None]
    second_member = jnp.logical_not(first_member) & (packed_buffer[None, :] <= N)
    degree = jnp.where(first_member, lower_wave[:, None] + packed_buffer[None, :], packed_buffer[None, :] - 1)
    degree = jnp.clip(degree, 0, N - 1).astype(jnp.int32)
    return (first_member, second_member, degree)

def reference(adjoint_grid, wind, legendre, vertical, pair_table, degree_matrix):
    wavenumbers = jnp.stack([pair_table, N - 1 - pair_table], axis=1).astype(jnp.int32)
    basis = fourier_basis(wavenumbers, LON)
    analysis_table = (basis * (1.0 / math.sqrt(LON))).astype(jnp.bfloat16)
    synthesis_table = (basis * (1.0 / math.sqrt(N))).astype(jnp.bfloat16)
    flattened = adjoint_grid.reshape(LEV * LAT, LON)
    fourier = jnp.dot(flattened, analysis_table.T, preferred_element_type=jnp.float32).astype(jnp.bfloat16)
    fourier = fourier.reshape(LEV, LAT, 4 * PAIRS).transpose(2, 0, 1)
    column = jnp.arange(4 * PAIRS, dtype=jnp.int32)
    lower_cols = pair_table[column // 4]
    member = column // 2 % 2
    first_member, second_member, degree = member_layout(lower_cols, 0, KP)
    own_rows = jnp.where((member == 0)[:, None], first_member, second_member).astype(jnp.float32)
    matrix_index = degree_matrix[degree]
    vertical_full = vertical.astype(jnp.float32)

    def one_column(operands):
        table_col, local_column, index_col, field_col = operands
        table_full = table_col.astype(jnp.float32)
        spectral_state = jnp.einsum('lk,vl->kv', table_full, field_col.astype(jnp.float32)) * local_column[:, None]
        spectral_half = lax.optimization_barrier(spectral_state.astype(jnp.bfloat16)).astype(jnp.float32)
        matrices = vertical_full[index_col]
        solved_columns = jnp.einsum('kv,kvo->ko', spectral_half, matrices)
        solved_half = lax.optimization_barrier(solved_columns.astype(jnp.bfloat16)).astype(jnp.float32)
        return jnp.einsum('lk,ko->ol', table_full, solved_half).astype(jnp.bfloat16)
    coeffs = lax.map(one_column, (legendre, own_rows, matrix_index, fourier))
    columns = coeffs.transpose(1, 2, 0).reshape(LEV * LAT, 4 * PAIRS)
    regridded = jnp.dot(columns, synthesis_table, preferred_element_type=jnp.float32).reshape(LEV, LAT, LON)
    return (regridded * wind.astype(jnp.float32)).astype(jnp.bfloat16)
```

```python
import math

import jax
import jax.numpy as jnp
from jax import lax
from jax.experimental import pallas as pl
from jax.experimental.pallas import tpu as pltpu
from jax.sharding import PartitionSpec as P

N = 512
LON = 1536
BF = jnp.bfloat16
F32 = jnp.float32
MESH = pl.DeviceIdType.MESH
NT = (((1,), (1,)), ((), ()))
TN = (((0,), (0,)), ((), ()))


def dot(a, b, dims=(((1,), (0,)), ((), ()))):
    return lax.dot_general(a, b, dims, preferred_element_type=F32)


def cosine(phase):
    w = (jnp.abs(phase - 0.5 * LON) - 0.25 * LON) * (2.0 * math.pi / LON)
    s = w * w
    p = -2.3889859e-08
    for c in (2.7525562e-06, -0.00019840874, 0.0083333310, -0.16666667):
        p = p * s + c
    return w + w * s * p


def wrap(phase):
    return phase - LON * jnp.floor(phase * (1.0 / LON))


def iota(shape, dim):
    return lax.broadcasted_iota(jnp.int32, shape, dim)


def build_table(pairs_row, scale, table, rows=64):
    pairs = table.shape[0] // 4
    spread = jnp.broadcast_to(pairs_row, (128, pairs)).astype(BF)

    @pl.loop(0, table.shape[0] // rows)
    def _(block):
        start = pl.multiple_of(block * rows, rows)
        pick = (start + iota((rows, pairs), 0)) // 4 == iota((rows, pairs), 1)
        lower = dot(pick.astype(F32).astype(BF), spread, NT)
        row = start + iota((rows, 128), 0)
        wave = jnp.where(row // 2 % 2 == 0, lower, N - 1.0 - lower)
        first = wave * iota((rows, 128), 1).astype(F32) + (row % 2).astype(F32) * (LON / 4)
        step = wave * 128.0
        now = cosine(wrap(first)) * scale
        later = cosine(wrap(first + step)) * scale
        twice = 2.0 * cosine(wrap(step))
        for a in range(LON // 128):
            table[pl.ds(start, rows), a * 128:(a + 1) * 128] = now.astype(BF)
            now, later = later, twice * later - now


def kernel(lats, levs, grid, wind, leg, vert, pairs_row, dm_row, pairs_s, out,
           table, wide, ls, lr, zs, zr, ys, yr, ks, kr, merged,
           ls_s, lr_s, zs_s, zr_s, ys_s, yr_s, ks_s, kr_s):
    me_lat, me_lev = lax.axis_index("lat"), lax.axis_index("lev")
    band = grid.shape[0] // 2
    chunks = zs.shape[0]
    barrier = pltpu.get_barrier_semaphore()

    @pl.loop(1, levs)
    def _(d):
        pl.semaphore_signal(barrier, inc=1, device_id={"lev": lax.rem(me_lev + d, levs)}, device_id_type=MESH)

    @pl.loop(1, lats)
    def _(d):
        pl.semaphore_signal(barrier, inc=1, device_id={"lat": lax.rem(me_lat + d, lats)}, device_id_type=MESH)

    build_table(pairs_row[...], 1.0 / math.sqrt(LON), table)
    low = iota((band, 128), 1) < 64
    for p in range(lats // 2):
        both = dot(grid[...], table[p * 128:(p + 1) * 128, :], NT)
        a, b = both[:band], both[band:]
        ls[2 * p] = jnp.where(low, a, pltpu.roll(b, 64, 1)).astype(BF)
        ls[2 * p + 1] = jnp.where(low, pltpu.roll(a, 64, 1), b).astype(BF)

    pl.semaphore_wait(barrier, levs + lats - 2)

    def lat_copy(src, dst, send, recv, t):
        return pltpu.make_async_remote_copy(src, dst, send, recv, device_id={"lat": t}, device_id_type=MESH)

    def lev_copy(src, dst, send, recv, t):
        return pltpu.make_async_remote_copy(src, dst, send, recv, device_id={"lev": t}, device_id_type=MESH)

    def lat_phase(src, dst, send, recv):
        @pl.loop(1, lats)
        def _(d):
            t = lax.rem(me_lat + d, lats)
            lat_copy(src.at[t], dst.at[me_lat], send, recv, t).start()
        dst[me_lat] = src[me_lat]

    def lat_wait(src, dst, send, recv):
        whole = lat_copy(src.at[pl.ds(0, lats - 1)], dst.at[pl.ds(0, lats - 1)], send, recv, me_lat)
        whole.wait_recv()
        whole.wait_send()

    def lev_phase(src, dst, send, recv):
        chips = levs // 2
        @pl.loop(0, levs)
        def _(s):
            k = chips - 1 - s // 2
            h = (k + 1) // 2
            dz = jnp.where(k % 2 == 1, h, chips - h)
            t = lax.rem(me_lev // 2 + dz, chips) * 2 + lax.rem(me_lev + s, 2)

            @pl.when(t != me_lev)
            def _():
                lev_copy(src.at[:, t], dst.at[:, me_lev], send, recv, t).start()
        for q in range(chunks):
            dst[q, me_lev] = src[q, me_lev]

    def lev_wait(src, dst, send, recv):
        whole = lev_copy(src.at[:, pl.ds(0, levs - 1)], dst.at[:, pl.ds(0, levs - 1)], send, recv, me_lev)
        whole.wait_recv()
        whole.wait_send()

    lat_phase(ls, lr, ls_s, lr_s)
    r, s = iota((128, 128), 0), iota((128, 128), 1)
    swap = (s == r % 2 * 64 + r // 2).astype(F32).astype(BF)
    lat_wait(ls, lr, ls_s, lr_s)

    turned = dot(swap, lr[...].reshape(lats * band, 128), NT)
    for q in range(chunks):
        zs[q] = turned[:, q * 128:(q + 1) * 128].astype(BF).reshape(64, 2, 128)
    lev_phase(zs, zr, zs_s, zr_s)

    build_table(pairs_row[...], 1.0 / math.sqrt(N), wide)
    rows = leg.shape[0]
    column = me_lat * levs + me_lev
    lower = pairs_s[column // 4]
    row = iota((rows, 1), 0)
    first = column // 2 % 2 == 0
    bound = N - lower
    own = jnp.where(first, (row < bound).astype(F32), ((row >= bound) & (row <= N)).astype(F32))
    degree = jnp.where(row < bound, lower + row, row - 1)
    degree = jnp.clip(degree, 0, N - 1)
    hit = degree == iota((rows, N), 1)
    index = jnp.sum(jnp.where(hit, dm_row[...].astype(F32), 0.0), axis=1, keepdims=True)
    lev_wait(zs, zr, zs_s, zr_s)

    field = jnp.concatenate([zr[q].reshape(128, 128) for q in range(chunks)], axis=1)
    spectral = dot(leg[...], field, NT) * own
    for op in range(vert.shape[0] // 128):
        merged[:, op * 128:(op + 1) * 128] = jnp.where(index == float(op), spectral, 0.0).astype(BF)
    solved = dot(merged[...], vert[...]).astype(BF)
    coeffs = dot(solved, leg[...], TN)
    for q in range(chunks):
        ys[q] = coeffs[:, q * 128:(q + 1) * 128].astype(BF).reshape(64, 2, 128)
    lev_phase(ys, yr, ys_s, yr_s)
    lev_wait(ys, yr, ys_s, yr_s)

    back = jnp.concatenate(
        [dot(yr[q].reshape(128, 128), swap, TN).astype(BF) for q in range(chunks)], axis=0)
    ks[...] = back.reshape(lats, band, 128)
    lat_phase(ks, kr, ks_s, kr_s)
    lat_wait(ks, kr, ks_s, kr_s)

    tops, ends = [], []
    for p in range(lats // 2):
        a, b = kr[2 * p].astype(F32), kr[2 * p + 1].astype(F32)
        tops.append(jnp.where(low, a, pltpu.roll(b, 64, 1)).astype(BF))
        ends.append(jnp.where(low, pltpu.roll(a, 64, 1), b).astype(BF))
    columns = jnp.concatenate([jnp.concatenate(tops, axis=1), jnp.concatenate(ends, axis=1)], axis=0)
    for x in range(LON // 256):
        cut = slice(x * 256, (x + 1) * 256)
        out[:, cut] = (dot(columns, wide[:, cut]) * wind[:, cut].astype(F32)).astype(BF)


def solution(mesh):
    lats, levs = mesh.shape["lat"], mesh.shape["lev"]

    def body(adjoint_grid, wind, legendre, vertical, pair_table, degree_matrix):
        levels, band, points = adjoint_grid.shape
        rows = legendre.shape[2]
        chunks = legendre.shape[1] // 128
        vmem = pl.BlockSpec(memory_space=pltpu.VMEM)
        smem = pl.BlockSpec(memory_space=pltpu.SMEM)
        lat_block = pltpu.VMEM((lats, band, 128), BF)
        lev_block = pltpu.VMEM((chunks, levs, 2, 128), BF)
        out = pl.pallas_call(
            lambda *refs: kernel(lats, levs, *refs),
            out_shape=jax.ShapeDtypeStruct((levels * band, points), BF),
            in_specs=[vmem] * 6 + [smem],
            out_specs=vmem,
            scratch_shapes=[pltpu.VMEM((4 * pair_table.shape[0], points), BF)] * 2
            + [lat_block] * 2 + [lev_block] * 4 + [lat_block] * 2
            + [pltpu.VMEM((rows, vertical.shape[0] * vertical.shape[1]), BF)]
            + [pltpu.SemaphoreType.DMA] * 8,
            compiler_params=pltpu.CompilerParams(
                collective_id=0, has_side_effects=True, vmem_limit_bytes=60 << 20),
            name="adjoint_step",
        )(
            adjoint_grid.reshape(levels * band, points),
            wind.reshape(levels * band, points),
            jnp.swapaxes(legendre, 1, 2).reshape(rows, legendre.shape[1]),
            vertical.reshape(-1, vertical.shape[2]),
            pair_table.reshape(1, -1),
            degree_matrix.reshape(1, -1),
            pair_table,
        )
        return out.reshape(levels, band, points)

    placed = (
        P("lev", "lat", None),
        P("lev", "lat", None),
        P(("lat", "lev"), None, None),
        P(),
        P(),
        P(),
    )
    return jax.shard_map(
        body, mesh=mesh, in_specs=placed, out_specs=P("lev", "lat", None), check_vma=False
    )
```

```python
import math

import jax
import jax.numpy as jnp
from jax import lax
from jax.experimental import pallas as pl
from jax.experimental.pallas import tpu as pltpu
from jax.sharding import PartitionSpec as P

N = 512
LON = 1536
BF = jnp.bfloat16
F32 = jnp.float32
MESH = pl.DeviceIdType.MESH
NT = (((1,), (1,)), ((), ()))
TN = (((0,), (0,)), ((), ()))


def dot(a, b, dims=(((1,), (0,)), ((), ()))):
    return lax.dot_general(a, b, dims, preferred_element_type=F32)


def cosine(phase):
    w = (jnp.abs(phase - 0.5 * LON) - 0.25 * LON) * (2.0 * math.pi / LON)
    s = w * w
    p = -2.3889859e-08
    for c in (2.7525562e-06, -0.00019840874, 0.0083333310, -0.16666667):
        p = p * s + c
    return w + w * s * p


def wrap(phase):
    return phase - LON * jnp.floor(phase * (1.0 / LON))


def iota(shape, dim):
    return lax.broadcasted_iota(jnp.int32, shape, dim)


def build_table(pairs_row, scale, table, rows=64):
    pairs = table.shape[0] // 4
    spread = jnp.broadcast_to(pairs_row, (128, pairs)).astype(BF)

    @pl.loop(0, table.shape[0] // rows)
    def _(block):
        start = pl.multiple_of(block * rows, rows)
        pick = (start + iota((rows, pairs), 0)) // 4 == iota((rows, pairs), 1)
        lower = dot(pick.astype(F32).astype(BF), spread, NT)
        row = start + iota((rows, 128), 0)
        wave = jnp.where(row // 2 % 2 == 0, lower, N - 1.0 - lower)
        first = wave * iota((rows, 128), 1).astype(F32) + (row % 2).astype(F32) * (LON / 4)
        step = wave * 128.0
        now = cosine(wrap(first)) * scale
        later = cosine(wrap(first + step)) * scale
        twice = 2.0 * cosine(wrap(step))
        for a in range(LON // 128):
            table[pl.ds(start, rows), a * 128:(a + 1) * 128] = now.astype(BF)
            now, later = later, twice * later - now


def kernel(lats, levs, grid, wind_h, leg_h, vert_h, pairs_row, dm_row, pairs_s, out,
           wind, leg, vert, table, wide, ls, lr, zs, zr, ys, yr, ks, kr, merged,
           ls_s, lr_s, zs_s, zr_s, ys_s, yr_s, ks_s, kr_s, load_s, plane_s, line_s):
    me_lat, me_lev = lax.axis_index("lat"), lax.axis_index("lev")
    band = grid.shape[0] // 2
    chunks = zs.shape[0]
    chips = levs // 2
    me_z, core = me_lev // 2, lax.rem(me_lev, 2)
    loads = [pltpu.make_async_copy(src, dst, load_s.at[n])
             for n, (src, dst) in enumerate(((leg_h, leg), (vert_h, vert), (wind_h, wind)))]
    for load in loads:
        load.start()

    barrier = pltpu.get_barrier_semaphore()

    @pl.loop(1, chips)
    def _(d):
        pl.semaphore_signal(barrier, inc=1, device_id={"lev": lax.rem(me_z + d, chips) * 2}, device_id_type=MESH)

    @pl.loop(1, lats)
    def _(d):
        pl.semaphore_signal(barrier, inc=1, device_id=(lax.rem(me_lat + d, lats), me_z * 2 + 1), device_id_type=MESH)

    @pl.when(core == 0)
    def _():
        pl.semaphore_signal(barrier, inc=1, device_id={"lev": me_lev + 1}, device_id_type=MESH)

    build_table(pairs_row[...], 1.0 / math.sqrt(LON), table)
    low = iota((band, 128), 1) < 64
    for p in range(lats // 2):
        both = dot(grid[...], table[p * 128:(p + 1) * 128, :], NT)
        a, b = both[:band], both[band:]
        ls[2 * p] = jnp.where(low, a, pltpu.roll(b, 64, 1)).astype(BF)
        ls[2 * p + 1] = jnp.where(low, pltpu.roll(a, 64, 1), b).astype(BF)

    @pl.when(core == 1)
    def _():
        pl.semaphore_wait(barrier, 2 * lats - 1)
        pl.semaphore_signal(plane_s, inc=1, device_id={"lev": me_lev - 1}, device_id_type=MESH)

    @pl.when(core == 0)
    def _():
        pl.semaphore_wait(plane_s, 1)

    def lat_copy(src, dst, send, recv, t):
        return pltpu.make_async_remote_copy(src, dst, send, recv, device_id={"lat": t}, device_id_type=MESH)

    def lev_copy(src, dst, send, recv, t):
        return pltpu.make_async_remote_copy(src, dst, send, recv, device_id={"lev": t}, device_id_type=MESH)

    def lat_phase(src, dst, send, recv):
        @pl.loop(1, lats)
        def _(d):
            t = lax.rem(me_lat + d, lats)
            lat_copy(src.at[t], dst.at[me_lat], send, recv, t).start()
        dst[me_lat] = src[me_lat]

    def lat_wait(src, dst, send, recv):
        whole = lat_copy(src.at[pl.ds(0, lats - 1)], dst.at[pl.ds(0, lats - 1)], send, recv, me_lat)
        whole.wait_recv()
        whole.wait_send()

    def lev_phase(src, dst, send, recv, waves):
        @pl.loop(0, levs)
        def _(s):
            k = chips - 1 - lax.rem(s, chips) if waves else chips - 1 - s // 2
            h = (k + 1) // 2
            dz = jnp.where(k % 2 == 1, h, chips - h)
            t = lax.rem(me_z + dz, chips) * 2 + (s // chips if waves else lax.rem(me_lev + s, 2))

            @pl.when(t != me_lev)
            def _():
                lev_copy(src.at[:, t], dst.at[:, me_lev], send, recv, t).start()
        for q in range(chunks):
            dst[q, me_lev] = src[q, me_lev]

    def lev_wait(src, dst, send, recv):
        whole = lev_copy(src.at[:, pl.ds(0, levs - 1)], dst.at[:, pl.ds(0, levs - 1)], send, recv, me_lev)
        whole.wait_recv()
        whole.wait_send()

    lat_phase(ls, lr, ls_s, lr_s)
    r, s = iota((128, 128), 0), iota((128, 128), 1)
    swap = (s == r % 2 * 64 + r // 2).astype(F32).astype(BF)
    lat_wait(ls, lr, ls_s, lr_s)

    turned = dot(swap, lr[...].reshape(lats * band, 128), NT)
    for q in range(chunks):
        zs[q] = turned[:, q * 128:(q + 1) * 128].astype(BF).reshape(64, 2, 128)

    @pl.when(core == 0)
    def _():
        pl.semaphore_wait(barrier, levs - 2)
        pl.semaphore_signal(line_s, inc=1, device_id={"lev": me_lev + 1}, device_id_type=MESH)

    @pl.when(core == 1)
    def _():
        pl.semaphore_wait(line_s, 1)

    lev_phase(zs, zr, zs_s, zr_s, True)

    build_table(pairs_row[...], 1.0 / math.sqrt(N), wide)
    rows = leg.shape[0]
    column = me_lat * levs + me_lev
    lower = pairs_s[column // 4]
    row = iota((rows, 1), 0)
    first = column // 2 % 2 == 0
    bound = N - lower
    own = jnp.where(first, (row < bound).astype(F32), ((row >= bound) & (row <= N)).astype(F32))
    degree = jnp.where(row < bound, lower + row, row - 1)
    degree = jnp.clip(degree, 0, N - 1)
    hit = degree == iota((rows, N), 1)
    index = jnp.sum(jnp.where(hit, dm_row[...].astype(F32), 0.0), axis=1, keepdims=True)
    for load in loads:
        load.wait()
    lev_wait(zs, zr, zs_s, zr_s)

    field = jnp.concatenate([zr[q].reshape(128, 128) for q in range(chunks)], axis=1)
    spectral = dot(leg[...], field, NT) * own
    for op in range(vert.shape[0] // 128):
        merged[:, op * 128:(op + 1) * 128] = jnp.where(index == float(op), spectral, 0.0).astype(BF)
    solved = dot(merged[...], vert[...]).astype(BF)
    coeffs = dot(solved, leg[...], TN)
    for q in range(chunks):
        ys[q] = coeffs[:, q * 128:(q + 1) * 128].astype(BF).reshape(64, 2, 128)
    lev_phase(ys, yr, ys_s, yr_s, False)
    lev_wait(ys, yr, ys_s, yr_s)

    back = jnp.concatenate(
        [dot(yr[q].reshape(128, 128), swap, TN).astype(BF) for q in range(chunks)], axis=0)
    ks[...] = back.reshape(lats, band, 128)
    lat_phase(ks, kr, ks_s, kr_s)
    lat_wait(ks, kr, ks_s, kr_s)

    tops, ends = [], []
    for p in range(lats // 2):
        a, b = kr[2 * p].astype(F32), kr[2 * p + 1].astype(F32)
        tops.append(jnp.where(low, a, pltpu.roll(b, 64, 1)).astype(BF))
        ends.append(jnp.where(low, pltpu.roll(a, 64, 1), b).astype(BF))
    columns = jnp.concatenate([jnp.concatenate(tops, axis=1), jnp.concatenate(ends, axis=1)], axis=0)
    for x in range(LON // 256):
        cut = slice(x * 256, (x + 1) * 256)
        out[:, cut] = (dot(columns, wide[:, cut]) * wind[:, cut].astype(F32)).astype(BF)


def solution(mesh):
    lats, levs = mesh.shape["lat"], mesh.shape["lev"]

    def body(adjoint_grid, wind, legendre, vertical, pair_table, degree_matrix):
        levels, band, points = adjoint_grid.shape
        rows = legendre.shape[2]
        chunks = legendre.shape[1] // 128
        vmem = pl.BlockSpec(memory_space=pltpu.VMEM)
        smem = pl.BlockSpec(memory_space=pltpu.SMEM)
        lat_block = pltpu.VMEM((lats, band, 128), BF)
        lev_block = pltpu.VMEM((chunks, levs, 2, 128), BF)
        out = pl.pallas_call(
            lambda *refs: kernel(lats, levs, *refs),
            out_shape=jax.ShapeDtypeStruct((levels * band, points), BF),
            in_specs=[vmem] + [pl.BlockSpec(memory_space=pl.ANY)] * 3 + [vmem] * 2 + [smem],
            out_specs=vmem,
            scratch_shapes=[
                pltpu.VMEM((levels * band, points), BF),
                pltpu.VMEM((rows, legendre.shape[1]), BF),
                pltpu.VMEM((vertical.shape[0] * vertical.shape[1], vertical.shape[2]), BF),
            ]
            + [pltpu.VMEM((4 * pair_table.shape[0], points), BF)] * 2
            + [lat_block] * 2 + [lev_block] * 4 + [lat_block] * 2
            + [pltpu.VMEM((rows, vertical.shape[0] * vertical.shape[1]), BF)]
            + [pltpu.SemaphoreType.DMA] * 8
            + [pltpu.SemaphoreType.DMA((3,)), pltpu.SemaphoreType.REGULAR, pltpu.SemaphoreType.REGULAR],
            compiler_params=pltpu.CompilerParams(
                collective_id=0, has_side_effects=True, vmem_limit_bytes=60 << 20),
            name="adjoint_step",
        )(
            adjoint_grid.reshape(levels * band, points),
            wind.reshape(levels * band, points),
            jnp.swapaxes(legendre, 1, 2).reshape(rows, legendre.shape[1]),
            vertical.reshape(-1, vertical.shape[2]),
            pair_table.reshape(1, -1),
            degree_matrix.reshape(1, -1),
            pair_table,
        )
        return out.reshape(levels, band, points)

    placed = (
        P("lev", "lat", None),
        P("lev", "lat", None),
        P(("lat", "lev"), None, None),
        P(),
        P(),
        P(),
    )
    return jax.shard_map(
        body, mesh=mesh, in_specs=placed, out_specs=P("lev", "lat", None), check_vma=False
    )
```

```python
import math

import jax
import jax.numpy as jnp
from jax import lax
from jax.experimental import pallas as pl
from jax.experimental.pallas import tpu as pltpu
from jax.sharding import PartitionSpec as P

N = 512
LON = 1536
BF = jnp.bfloat16
F32 = jnp.float32
MESH = pl.DeviceIdType.MESH
NT = (((1,), (1,)), ((), ()))
TN = (((0,), (0,)), ((), ()))


def dot(a, b, dims=(((1,), (0,)), ((), ()))):
    return lax.dot_general(a, b, dims, preferred_element_type=F32)


def cosine(phase):
    w = (jnp.abs(phase - 0.5 * LON) - 0.25 * LON) * (2.0 * math.pi / LON)
    s = w * w
    p = -2.3889859e-08
    for c in (2.7525562e-06, -0.00019840874, 0.0083333310, -0.16666667):
        p = p * s + c
    return w + w * s * p


def wrap(phase):
    return phase - LON * jnp.floor(phase * (1.0 / LON))


def iota(shape, dim):
    return lax.broadcasted_iota(jnp.int32, shape, dim)


def waves_of(pairs_row, waves):
    rows, pairs = waves.shape[0], pairs_row.shape[1]
    spread = jnp.broadcast_to(pairs_row, (128, pairs)).astype(BF)
    pick = iota((rows, pairs), 0) // 4 == iota((rows, pairs), 1)
    lower = dot(pick.astype(F32).astype(BF), spread, NT)
    waves[...] = jnp.where(iota((rows, 128), 0) // 2 % 2 == 0, lower, N - 1.0 - lower)


def table_rows(waves, scale, table, start, rows):
    wave = waves[pl.ds(start, rows), :]
    quarter = (iota((rows, 128), 0) % 2).astype(F32) * (LON / 4)
    first = wave * iota((rows, 128), 1).astype(F32) + quarter
    step = wave * 128.0
    now = cosine(wrap(first)) * scale
    later = cosine(wrap(first + step)) * scale
    twice = 2.0 * cosine(wrap(step))
    sign = 1.0 - 2.0 * (wave - 2.0 * jnp.floor(wave * 0.5))
    half = LON // 256
    for a in range(half):
        table[pl.ds(start, rows), a * 128:(a + 1) * 128] = now.astype(BF)
        table[pl.ds(start, rows), (half + a) * 128:(half + a + 1) * 128] = (now * sign).astype(BF)
        now, later = later, twice * later - now


def kernel(lats, levs, grid_h, wind_h, leg_h, vert_h, pairs_h, dm_h, flat_h,
           columns, wide, wind, pairs_row, dm_row, pairs_s, grid, leg, vert, table, waves, ls, lr, zs, zr, ys, yr, ks, kr, merged, masks, paired,
           ls_s, lr_s, zs_s, zr_s, ys_s, yr_s, ks_s, kr_s, load_s, plane_s, line_s):
    me_lat, me_lev = lax.axis_index("lat"), lax.axis_index("lev")
    band = grid_h.shape[0] // 2
    chunks = zs.shape[0]
    chips = levs // 2
    me_z, core = me_lev // 2, lax.rem(me_lev, 2)
    loads = [pltpu.make_async_copy(src, dst, load_s.at[n])
             for n, (src, dst) in enumerate((
                 (pairs_h, pairs_row), (grid_h, grid), (flat_h, pairs_s), (dm_h, dm_row),
                 (leg_h, leg), (vert_h, vert), (wind_h, wind)))]

    barrier = pltpu.get_barrier_semaphore()

    @pl.loop(0, chips - 1)
    def _(k):
        h = (chips - k) // 2
        z = lax.rem(me_z + jnp.where(lax.rem(k, 2) == 0, h, chips - h), chips)
        pl.semaphore_signal(barrier, inc=1, device_id={"lev": z * 2}, device_id_type=MESH)

    @pl.loop(1, lats)
    def _(d):
        pl.semaphore_signal(barrier, inc=1, device_id=(lax.rem(me_lat + d, lats), me_z * 2 + 1), device_id_type=MESH)

    @pl.when(core == 0)
    def _():
        pl.semaphore_signal(barrier, inc=1, device_id={"lev": me_lev + 1}, device_id_type=MESH)

    for load in loads:
        load.start()
    loads[0].wait()
    waves_of(pairs_row[...], waves)
    low = iota((band, 128), 1) < 64

    def transform(p):
        both = dot(grid[...], table[p * 128:(p + 1) * 128, :], NT)
        a, b = both[:band], both[band:]
        ls[2 * p] = jnp.where(low, a, pltpu.roll(b, 64, 1)).astype(BF)
        ls[2 * p + 1] = jnp.where(low, pltpu.roll(a, 64, 1), b).astype(BF)

    loads[1].wait()
    for p in range(lats // 2):
        table_rows(waves, 1.0 / math.sqrt(LON), table, p * 128, 128)
        if p > 0:
            transform(p - 1)
    transform(lats // 2 - 1)

    @pl.when(core == 1)
    def _():
        pl.semaphore_wait(barrier, 2 * lats - 1)
        pl.semaphore_signal(plane_s, inc=1, device_id={"lev": me_lev - 1}, device_id_type=MESH)

    @pl.when(core == 0)
    def _():
        pl.semaphore_wait(plane_s, 1)

    def lat_copy(src, dst, send, recv, t):
        return pltpu.make_async_remote_copy(src, dst, send, recv, device_id={"lat": t}, device_id_type=MESH)

    def lev_copy(src, dst, send, recv, t):
        return pltpu.make_async_remote_copy(src, dst, send, recv, device_id={"lev": t}, device_id_type=MESH)

    def lat_phase(src, dst, send, recv):
        width = math.isqrt(lats)
        steps = [(dy, dx) for dy in range(width) for dx in range(width) if dy or dx]
        steps.sort(key=lambda step: -sum(min(d, width - d) for d in step))
        for dy, dx in steps:
            t = lax.rem(me_lat // width + dy, width) * width + lax.rem(me_lat + dx, width)
            lat_copy(src.at[t], dst.at[me_lat], send, recv, t).start()
        dst[me_lat] = src[me_lat]

    def lat_wait(src, dst, send, recv):
        whole = lat_copy(src.at[pl.ds(0, lats - 1)], dst.at[pl.ds(0, lats - 1)], send, recv, me_lat)
        whole.wait_recv()
        whole.wait_send()

    def lev_phase(src, dst, send, recv, waves):
        @pl.loop(0, levs)
        def _(s):
            k = chips - 1 - lax.rem(s, chips) if waves else chips - 1 - s // 2
            h = (k + 1) // 2
            dz = jnp.where(k % 2 == 1, h, chips - h)
            t = lax.rem(me_z + dz, chips) * 2 + (s // chips if waves else lax.rem(me_lev + s, 2))

            @pl.when(t != me_lev)
            def _():
                lev_copy(src.at[:, t], dst.at[:, me_lev], send, recv, t).start()
        for q in range(chunks):
            dst[q, me_lev] = src[q, me_lev]

    def lev_wait(src, dst, send, recv):
        whole = lev_copy(src.at[:, pl.ds(0, levs - 1)], dst.at[:, pl.ds(0, levs - 1)], send, recv, me_lev)
        whole.wait_recv()
        whole.wait_send()

    lat_phase(ls, lr, ls_s, lr_s)
    r, s = iota((128, 128), 0), iota((128, 128), 1)
    swap = (s == r % 2 * 64 + r // 2).astype(F32).astype(BF)
    lat_wait(ls, lr, ls_s, lr_s)

    turned = dot(swap, lr[...].reshape(lats * band, 128), NT)
    for q in range(chunks):
        zs[q] = turned[:, q * 128:(q + 1) * 128].astype(BF).reshape(64, 2, 128)

    @pl.when(core == 0)
    def _():
        pl.semaphore_wait(barrier, levs - 2)
        pl.semaphore_signal(line_s, inc=1, device_id={"lev": me_lev + 1}, device_id_type=MESH)

    @pl.when(core == 1)
    def _():
        pl.semaphore_wait(line_s, 1)

    lev_phase(zs, zr, zs_s, zr_s, True)

    @pl.loop(0, wide.shape[0] // 128)
    def _(block):
        table_rows(waves, 1.0 / math.sqrt(N), wide, pl.multiple_of(block * 128, 128), 128)

    rows = leg_h.shape[0]
    column = me_lat * levs + me_lev
    for load in loads[2:]:
        load.wait()
    lower = pairs_s[column // 4]
    row = iota((rows, 1), 0)
    first = column // 2 % 2 == 0
    bound = N - lower
    own = jnp.where(first, (row < bound).astype(F32), ((row >= bound) & (row <= N)).astype(F32))
    degree = jnp.where(row < bound, lower + row, row - 1)
    degree = jnp.clip(degree, 0, N - 1)
    hit = degree == iota((rows, N), 1)
    index = jnp.sum(jnp.where(hit, dm_row[...].astype(F32), 0.0), axis=1, keepdims=True)
    slots = vert_h.shape[0] // 256
    slot = jnp.floor(index * 0.5)
    for n in range(slots):
        chosen = jnp.where(slot == float(n), own, 0.0)
        masks[:, n * 128:(n + 1) * 128] = jnp.broadcast_to(chosen, (rows, 128)).astype(BF)
        for h in range(2):
            paired[n * 128:(n + 1) * 128, h * 128:(h + 1) * 128] = vert[(2 * n + h) * 128:(2 * n + h + 1) * 128, :]
    lev_wait(zs, zr, zs_s, zr_s)

    field = jnp.concatenate([zr[q].reshape(128, 128) for q in range(chunks)], axis=1)
    spectral = dot(leg[...], field, NT).astype(BF)
    for n in range(slots):
        cut = slice(n * 128, (n + 1) * 128)
        merged[:, cut] = spectral * masks[:, cut]
    both = dot(merged[...], paired[...])
    solved = jnp.where(index == 2.0 * slot, both[:, :128], both[:, 128:]).astype(BF)
    coeffs = dot(solved, leg[...], TN)
    for q in range(chunks):
        ys[q] = coeffs[:, q * 128:(q + 1) * 128].astype(BF).reshape(64, 2, 128)
    lev_phase(ys, yr, ys_s, yr_s, False)
    lev_wait(ys, yr, ys_s, yr_s)

    back = jnp.concatenate(
        [dot(yr[q].reshape(128, 128), swap, TN).astype(BF) for q in range(chunks)], axis=0)
    ks[...] = back.reshape(lats, band, 128)
    lat_phase(ks, kr, ks_s, kr_s)
    lat_wait(ks, kr, ks_s, kr_s)

    tops, ends = [], []
    for p in range(lats // 2):
        a, b = kr[2 * p].astype(F32), kr[2 * p + 1].astype(F32)
        tops.append(jnp.where(low, a, pltpu.roll(b, 64, 1)).astype(BF))
        ends.append(jnp.where(low, pltpu.roll(a, 64, 1), b).astype(BF))
    columns[...] = jnp.concatenate([jnp.concatenate(tops, axis=1), jnp.concatenate(ends, axis=1)], axis=0)


def synthesis(columns, wide, wind, out):
    for x in range(LON // 256):
        cut = slice(x * 256, (x + 1) * 256)
        out[:, cut] = (dot(columns[...], wide[:, cut]) * wind[:, cut].astype(F32)).astype(BF)


def solution(mesh):
    lats, levs = mesh.shape["lat"], mesh.shape["lev"]

    def body(adjoint_grid, wind, legendre, vertical, pair_table, degree_matrix):
        levels, band, points = adjoint_grid.shape
        rows = legendre.shape[2]
        chunks = legendre.shape[1] // 128
        vmem = pl.BlockSpec(memory_space=pltpu.VMEM)
        lat_block = pltpu.VMEM((lats, band, 128), BF)
        lev_block = pltpu.VMEM((chunks, levs, 2, 128), BF)
        parts = pl.pallas_call(
            lambda *refs: kernel(lats, levs, *refs),
            out_shape=[
                jax.ShapeDtypeStruct((levels * band, 4 * pair_table.shape[0]), BF),
                jax.ShapeDtypeStruct((4 * pair_table.shape[0], points), BF),
                jax.ShapeDtypeStruct((levels * band, points), BF),
            ],
            in_specs=[pl.BlockSpec(memory_space=pl.ANY)] * 7,
            out_specs=[vmem] * 3,
            scratch_shapes=[
                pltpu.VMEM((1, pair_table.shape[0]), jnp.int32),
                pltpu.VMEM((1, degree_matrix.shape[0]), jnp.int32),
                pltpu.SMEM(pair_table.shape, jnp.int32),
                pltpu.VMEM((levels * band, points), BF),
                pltpu.VMEM((rows, legendre.shape[1]), BF),
                pltpu.VMEM((vertical.shape[0] * vertical.shape[1], vertical.shape[2]), BF),
            ]
            + [pltpu.VMEM((4 * pair_table.shape[0], points), BF)]
            + [pltpu.VMEM((4 * pair_table.shape[0], 128), F32)]
            + [lat_block] * 2 + [lev_block] * 4 + [lat_block] * 2
            + [pltpu.VMEM((rows, vertical.shape[0] // 2 * vertical.shape[1]), BF)] * 2
            + [pltpu.VMEM((vertical.shape[0] // 2 * vertical.shape[1], 2 * vertical.shape[2]), BF)]
            + [pltpu.SemaphoreType.DMA] * 8
            + [pltpu.SemaphoreType.DMA((7,)), pltpu.SemaphoreType.REGULAR, pltpu.SemaphoreType.REGULAR],
            compiler_params=pltpu.CompilerParams(
                collective_id=0, has_side_effects=True, vmem_limit_bytes=32 << 20),
            name="adjoint_step",
        )(*[pltpu.with_memory_space_constraint(array, pltpu.HBM) for array in (
            adjoint_grid.reshape(levels * band, points),
            wind.reshape(levels * band, points),
            jnp.swapaxes(legendre, 1, 2).reshape(rows, legendre.shape[1]),
            vertical.reshape(-1, vertical.shape[2]),
            pair_table.reshape(1, -1),
            degree_matrix.reshape(1, -1),
            pair_table,
        )])
        out = pl.pallas_call(
            synthesis,
            out_shape=jax.ShapeDtypeStruct((levels * band, points), BF),
            in_specs=[vmem] * 3,
            out_specs=vmem,
            compiler_params=pltpu.CompilerParams(vmem_limit_bytes=12 << 20),
            name="synthesis",
        )(*parts)
        return out.reshape(levels, band, points)

    placed = (
        P("lev", "lat", None),
        P("lev", "lat", None),
        P(("lat", "lev"), None, None),
        P(),
        P(),
        P(),
    )
    return jax.shard_map(
        body, mesh=mesh, in_specs=placed, out_specs=P("lev", "lat", None), check_vma=False
    )
```

```python
import math

import jax
import jax.numpy as jnp
from jax import lax
from jax.experimental import pallas as pl
from jax.experimental.pallas import tpu as pltpu
from jax.sharding import PartitionSpec as P

N = 512
LON = 1536
BF = jnp.bfloat16
F32 = jnp.float32
MESH = pl.DeviceIdType.MESH
NT = (((1,), (1,)), ((), ()))
TN = (((0,), (0,)), ((), ()))


def dot(a, b, dims=(((1,), (0,)), ((), ()))):
    return lax.dot_general(a, b, dims, preferred_element_type=F32)


def cosine(phase):
    w = (jnp.abs(phase - 0.5 * LON) - 0.25 * LON) * (2.0 * math.pi / LON)
    s = w * w
    p = -2.3889859e-08
    for c in (2.7525562e-06, -0.00019840874, 0.0083333310, -0.16666667):
        p = p * s + c
    return w + w * s * p


def wrap(phase):
    return phase - LON * jnp.floor(phase * (1.0 / LON))


def iota(shape, dim):
    return lax.broadcasted_iota(jnp.int32, shape, dim)


def waves_of(pairs_row, waves):
    rows, pairs = waves.shape[0], pairs_row.shape[1]
    spread = jnp.broadcast_to(pairs_row, (128, pairs)).astype(BF)
    pick = iota((rows, pairs), 0) // 4 == iota((rows, pairs), 1)
    lower = dot(pick.astype(F32).astype(BF), spread, NT)
    waves[...] = jnp.where(iota((rows, 128), 0) // 2 % 2 == 0, lower, N - 1.0 - lower)


def table_rows(waves, scale, table, start, rows):
    wave = waves[pl.ds(start, rows), :]
    quarter = (iota((rows, 128), 0) % 2).astype(F32) * (LON / 4)
    first = wave * iota((rows, 128), 1).astype(F32) + quarter
    step = wave * 128.0
    now = cosine(wrap(first)) * scale
    later = cosine(wrap(first + step)) * scale
    twice = 2.0 * cosine(wrap(step))
    sign = 1.0 - 2.0 * (wave - 2.0 * jnp.floor(wave * 0.5))
    half = LON // 256
    for a in range(half):
        table[pl.ds(start, rows), a * 128:(a + 1) * 128] = now.astype(BF)
        table[pl.ds(start, rows), (half + a) * 128:(half + a + 1) * 128] = (now * sign).astype(BF)
        now, later = later, twice * later - now


def kernel(lats, levs, grid_h, wind_h, leg_h, vert_h, pairs_h, dm_h, flat_h,
           columns, wide, wind, pairs_row, dm_row, pairs_s, grid, leg, vert, table, waves, ls, lr, zs, zr, ys, yr, ks, kr, merged, masks, paired,
           ls_s, lr_s, zs_s, zr_s, ys_s, yr_s, ks_s, kr_s, load_s, plane_s, line_s):
    me_lat, me_lev = lax.axis_index("lat"), lax.axis_index("lev")
    band = grid_h.shape[0] // 2
    chunks = zs.shape[0]
    chips = levs // 2
    me_z, core = me_lev // 2, lax.rem(me_lev, 2)
    loads = [pltpu.make_async_copy(src, dst, load_s.at[n])
             for n, (src, dst) in enumerate((
                 (pairs_h, pairs_row), (grid_h, grid), (flat_h, pairs_s), (dm_h, dm_row),
                 (leg_h, leg), (vert_h, vert), (wind_h, wind)))]

    barrier = pltpu.get_barrier_semaphore()

    @pl.loop(0, chips - 1)
    def _(k):
        h = (chips - k) // 2
        z = lax.rem(me_z + jnp.where(lax.rem(k, 2) == 0, h, chips - h), chips)
        pl.semaphore_signal(barrier, inc=1, device_id={"lev": z * 2}, device_id_type=MESH)

    @pl.loop(1, lats)
    def _(d):
        pl.semaphore_signal(barrier, inc=1, device_id=(lax.rem(me_lat + d, lats), me_z * 2 + 1), device_id_type=MESH)

    @pl.when(core == 0)
    def _():
        pl.semaphore_signal(barrier, inc=1, device_id={"lev": me_lev + 1}, device_id_type=MESH)

    for load in loads:
        load.start()
    loads[0].wait()
    waves_of(pairs_row[...], waves)
    low = iota((band, 128), 1) < 64

    def transform(p):
        both = dot(grid[...], table[p * 128:(p + 1) * 128, :], NT)
        a, b = both[:band], both[band:]
        ls[2 * p] = jnp.where(low, a, pltpu.roll(b, 64, 1)).astype(BF)
        ls[2 * p + 1] = jnp.where(low, pltpu.roll(a, 64, 1), b).astype(BF)

    loads[1].wait()
    for p in range(lats // 2):
        table_rows(waves, 1.0 / math.sqrt(LON), table, p * 128, 128)
        if p > 0:
            transform(p - 1)
    transform(lats // 2 - 1)

    @pl.when(core == 1)
    def _():
        pl.semaphore_wait(barrier, 2 * lats - 1)
        pl.semaphore_signal(plane_s, inc=1, device_id={"lev": me_lev - 1}, device_id_type=MESH)

    @pl.when(core == 0)
    def _():
        pl.semaphore_wait(plane_s, 1)

    def lat_copy(src, dst, send, recv, t):
        return pltpu.make_async_remote_copy(src, dst, send, recv, device_id={"lat": t}, device_id_type=MESH)

    def lev_copy(src, dst, send, recv, t):
        return pltpu.make_async_remote_copy(src, dst, send, recv, device_id={"lev": t}, device_id_type=MESH)

    def lat_phase(src, dst, send, recv):
        width = math.isqrt(lats)
        steps = [(dy, dx) for dy in range(width) for dx in range(width) if dy or dx]
        steps.sort(key=lambda step: -sum(min(d, width - d) for d in step))
        for dy, dx in steps:
            t = lax.rem(me_lat // width + dy, width) * width + lax.rem(me_lat + dx, width)
            lat_copy(src.at[t], dst.at[me_lat], send, recv, t).start()
        dst[me_lat] = src[me_lat]

    def lat_wait(src, dst, send, recv):
        whole = lat_copy(src.at[pl.ds(0, lats - 1)], dst.at[pl.ds(0, lats - 1)], send, recv, me_lat)
        whole.wait_recv()
        whole.wait_send()

    def lev_phase(src, dst, send, recv, waves):
        @pl.loop(0, levs)
        def _(s):
            k = chips - 1 - lax.rem(s, chips) if waves else chips - 1 - s // 2
            h = (k + 1) // 2
            dz = jnp.where(k % 2 == 1, h, chips - h)
            t = lax.rem(me_z + dz, chips) * 2 + (s // chips if waves else lax.rem(me_lev + s, 2))

            @pl.when(t != me_lev)
            def _():
                lev_copy(src.at[:, t], dst.at[:, me_lev], send, recv, t).start()
        for q in range(chunks):
            dst[q, me_lev] = src[q, me_lev]

    def lev_wait(src, dst, send, recv):
        whole = lev_copy(src.at[:, pl.ds(0, levs - 1)], dst.at[:, pl.ds(0, levs - 1)], send, recv, me_lev)
        whole.wait_recv()
        whole.wait_send()

    lat_phase(ls, lr, ls_s, lr_s)
    r, s = iota((128, 128), 0), iota((128, 128), 1)
    swap = (s == r % 2 * 64 + r // 2).astype(F32).astype(BF)
    lat_wait(ls, lr, ls_s, lr_s)

    turned = dot(swap, lr[...].reshape(lats * band, 128), NT)
    for q in range(chunks):
        zs[q] = turned[:, q * 128:(q + 1) * 128].astype(BF).reshape(64, 2, 128)

    @pl.when(core == 0)
    def _():
        pl.semaphore_wait(barrier, levs - 2)
        pl.semaphore_signal(line_s, inc=1, device_id={"lev": me_lev + 1}, device_id_type=MESH)

    @pl.when(core == 1)
    def _():
        pl.semaphore_wait(line_s, 1)

    lev_phase(zs, zr, zs_s, zr_s, True)

    @pl.loop(0, wide.shape[0] // 128)
    def _(block):
        table_rows(waves, 1.0 / math.sqrt(N), wide, pl.multiple_of(block * 128, 128), 128)

    rows = leg_h.shape[0]
    column = me_lat * levs + me_lev
    for load in loads[2:]:
        load.wait()
    lower = pairs_s[column // 4]
    row = iota((rows, 1), 0)
    first = column // 2 % 2 == 0
    bound = N - lower
    own = jnp.where(first, (row < bound).astype(F32), ((row >= bound) & (row <= N)).astype(F32))
    degree = jnp.where(row < bound, lower + row, row - 1)
    degree = jnp.clip(degree, 0, N - 1)
    hit = degree == iota((rows, N), 1)
    index = jnp.sum(jnp.where(hit, dm_row[...].astype(F32), 0.0), axis=1, keepdims=True)
    slots = vert_h.shape[0] // 256
    slot = jnp.floor(index * 0.5)
    for n in range(slots):
        chosen = jnp.where(slot == float(n), own, 0.0)
        masks[:, n * 128:(n + 1) * 128] = jnp.broadcast_to(chosen, (rows, 128)).astype(BF)
        for h in range(2):
            paired[n * 128:(n + 1) * 128, h * 128:(h + 1) * 128] = vert[(2 * n + h) * 128:(2 * n + h + 1) * 128, :]
    lev_wait(zs, zr, zs_s, zr_s)

    field = jnp.concatenate([zr[q].reshape(128, 128) for q in range(chunks)], axis=1)
    spectral = dot(leg[...], field, NT).astype(BF)
    for n in range(slots):
        cut = slice(n * 128, (n + 1) * 128)
        merged[:, cut] = spectral * masks[:, cut]
    both = dot(merged[...], paired[...])
    solved = jnp.where(index == 2.0 * slot, both[:, :128], both[:, 128:]).astype(BF)
    coeffs = dot(solved, leg[...], TN)
    for q in range(chunks):
        ys[q] = coeffs[:, q * 128:(q + 1) * 128].astype(BF).reshape(64, 2, 128)
    lev_phase(ys, yr, ys_s, yr_s, False)
    lev_wait(ys, yr, ys_s, yr_s)

    back = jnp.concatenate(
        [dot(yr[q].reshape(128, 128), swap, TN).astype(BF) for q in range(chunks)], axis=0)
    ks[...] = back.reshape(lats, band, 128)
    lat_phase(ks, kr, ks_s, kr_s)
    lat_wait(ks, kr, ks_s, kr_s)

    tops, ends = [], []
    for p in range(lats // 2):
        a, b = kr[2 * p].astype(F32), kr[2 * p + 1].astype(F32)
        tops.append(jnp.where(low, a, pltpu.roll(b, 64, 1)).astype(BF))
        ends.append(jnp.where(low, pltpu.roll(a, 64, 1), b).astype(BF))
    columns[...] = jnp.concatenate([jnp.concatenate(tops, axis=1), jnp.concatenate(ends, axis=1)], axis=0)


def synthesis(columns, wide, wind, out, part, sems):
    copies = []
    width = part.shape[2]
    for n in range(part.shape[0]):
        cut = slice(n * width, (n + 1) * width)
        part[n] = (dot(columns[...], wide[:, cut]) * wind[:, cut].astype(F32)).astype(BF)
        copies.append(pltpu.make_async_copy(part.at[n], out.at[:, cut], sems.at[n]))
        copies[-1].start()
    for copy in copies:
        copy.wait()


def solution(mesh):
    lats, levs = mesh.shape["lat"], mesh.shape["lev"]

    def body(adjoint_grid, wind, legendre, vertical, pair_table, degree_matrix):
        levels, band, points = adjoint_grid.shape
        rows = legendre.shape[2]
        chunks = legendre.shape[1] // 128
        vmem = pl.BlockSpec(memory_space=pltpu.VMEM)
        lat_block = pltpu.VMEM((lats, band, 128), BF)
        lev_block = pltpu.VMEM((chunks, levs, 2, 128), BF)
        parts = pl.pallas_call(
            lambda *refs: kernel(lats, levs, *refs),
            out_shape=[
                jax.ShapeDtypeStruct((levels * band, 4 * pair_table.shape[0]), BF),
                jax.ShapeDtypeStruct((4 * pair_table.shape[0], points), BF),
                jax.ShapeDtypeStruct((levels * band, points), BF),
            ],
            in_specs=[pl.BlockSpec(memory_space=pl.ANY)] * 7,
            out_specs=[vmem] * 3,
            scratch_shapes=[
                pltpu.VMEM((1, pair_table.shape[0]), jnp.int32),
                pltpu.VMEM((1, degree_matrix.shape[0]), jnp.int32),
                pltpu.SMEM(pair_table.shape, jnp.int32),
                pltpu.VMEM((levels * band, points), BF),
                pltpu.VMEM((rows, legendre.shape[1]), BF),
                pltpu.VMEM((vertical.shape[0] * vertical.shape[1], vertical.shape[2]), BF),
            ]
            + [pltpu.VMEM((4 * pair_table.shape[0], points), BF)]
            + [pltpu.VMEM((4 * pair_table.shape[0], 128), F32)]
            + [lat_block] * 2 + [lev_block] * 4 + [lat_block] * 2
            + [pltpu.VMEM((rows, vertical.shape[0] // 2 * vertical.shape[1]), BF)] * 2
            + [pltpu.VMEM((vertical.shape[0] // 2 * vertical.shape[1], 2 * vertical.shape[2]), BF)]
            + [pltpu.SemaphoreType.DMA] * 8
            + [pltpu.SemaphoreType.DMA((7,)), pltpu.SemaphoreType.REGULAR, pltpu.SemaphoreType.REGULAR],
            compiler_params=pltpu.CompilerParams(
                collective_id=0, has_side_effects=True, vmem_limit_bytes=32 << 20),
            name="adjoint_step",
        )(*[pltpu.with_memory_space_constraint(array, pltpu.HBM) for array in (
            adjoint_grid.reshape(levels * band, points),
            wind.reshape(levels * band, points),
            jnp.swapaxes(legendre, 1, 2).reshape(rows, legendre.shape[1]),
            vertical.reshape(-1, vertical.shape[2]),
            pair_table.reshape(1, -1),
            degree_matrix.reshape(1, -1),
            pair_table,
        )])
        out = pl.pallas_call(
            synthesis,
            out_shape=jax.ShapeDtypeStruct((levels * band, points), BF),
            in_specs=[vmem] * 3,
            out_specs=pl.BlockSpec(memory_space=pl.ANY),
            scratch_shapes=[
                pltpu.VMEM((points // 256, levels * band, 256), BF),
                pltpu.SemaphoreType.DMA((points // 256,)),
            ],
            compiler_params=pltpu.CompilerParams(vmem_limit_bytes=12 << 20),
            name="synthesis",
        )(*parts)
        return out.reshape(levels, band, points)

    placed = (
        P("lev", "lat", None),
        P("lev", "lat", None),
        P(("lat", "lev"), None, None),
        P(),
        P(),
        P(),
    )
    return jax.shard_map(
        body, mesh=mesh, in_specs=placed, out_specs=P("lev", "lat", None), check_vma=False
    )
```
